32 devices in a mesh: dp: 4 (over y, x), tensor: 8 (over z, core).
Axes of the slice: x: 2, y: 2, z: 4, core: 2. Of those that a mesh axis runs over, the one named last changes fastest.
Arguments:
- out_grad: bfloat16 [512, 4096], P('dp'), may hold values from -0.625 to 0.625
- gate_pre: bfloat16 [512, 16384], P('dp', 'tensor'), may hold values from -8 to 8
- up_pre: bfloat16 [512, 16384], P('dp', 'tensor'), may hold values from -6 to 6
- rotated_codes: int32 [512, 16384], P('dp', 'tensor'), may hold values from -127 to 127
- rotated_scale: float32 [512], P('dp'), may hold values from 0.002 to 0.02
- input_codes: int32 [512, 4096], P('tensor', 'dp'), may hold values from -127 to 127
- input_scale: float32 [512], P('tensor'), may hold values from 0.004 to 0.04
- gate_codes: int32 [4096, 16384], P('dp', 'tensor'), may hold values from -127 to 127
- gate_scale: float32 [16384], P('tensor'), may hold values from 7e-05 to 0.0007
- up_codes: int32 [4096, 16384], P('dp', 'tensor'), may hold values from -127 to 127
- up_scale: float32 [16384], P('tensor'), may hold values from 7e-05 to 0.0007
- down_codes: int32 [16384, 4096], P('tensor', 'dp'), may hold values from -127 to 127
- down_scale: float32 [4096], P('dp'), may hold values from 7e-05 to 0.0007
- sign_bits: int32 [16384], P('tensor'), may hold values from 0 to 1
Outputs:
- grad_down: bfloat16 [16384, 4096], P('tensor', 'dp')
- grad_gate: bfloat16 [4096, 16384], P('dp', 'tensor')
- grad_up: bfloat16 [4096, 16384], P('dp', 'tensor')
- grad_input: bfloat16 [512, 4096], P('tensor', 'dp')
The draws below stay inside these ranges and needn't reach their ends.
Inputs may be any that keep to these rules, and one draw needn't show every extreme that they name: `rotated_codes`: quantized codes of the rotated hidden activations. `input_codes`: quantized codes of the layer input. `gate_codes`: quantized codes of the gate projection. `up_codes`: quantized codes of the up projection. `down_codes`: quantized codes of the down projection.
All inputs are finite; a program needn't handle non-finite values.
Results may differ from the reference program's by a relative error of at most 0.017.
Values may be sent and summed in bfloat16 or wider, within the bound.
No kernel may reach another device: no remote copies, remote signals or barrier semaphores. Data moves between devices by JAX's collectives and lax.ppermute only.
A program may use at most 128 MiB of HBM per device.

```python
import math
import jax
import jax.numpy as jnp
from jax import lax

D = 4096
F = 16384
TOKENS = 512
FEAT_BLOCK = 1024
UNIT_BLOCK = 2048
N_DP = 4
N_TENSOR = 8


def with_ends(drawn, rng, low, top_value):
    place = [jax.random.randint(jax.random.fold_in(rng, axis), (), 0, length) for axis, length in enumerate(drawn.shape)]
    widest = drawn.shape.index(max(drawn.shape))
    neighbour = place[:widest] + [(place[widest] + 1) % drawn.shape[widest]] + place[widest + 1:]
    return drawn.at[tuple(place)].set(low).at[tuple(neighbour)].set(top_value)


def level_of(key, shape, shards, low, top_value):
    level, own = 1.0, jax.random.fold_in(key, 6)
    for axis_at, parts in shards:
        steps = jnp.exp(jax.random.uniform(jax.random.fold_in(own, axis_at), (parts,), jnp.float32, low / len(shards), top_value / len(shards)))
        level = level * jnp.repeat(steps, shape[axis_at] // parts).reshape([-1 if axis == axis_at else 1 for axis in range(len(shape))])
    return level


def gaussian(key, dims, deviation, bound, cuts=(), kind=jnp.bfloat16):
    values = jax.random.normal(key, dims, jnp.float32) * deviation
    if len(cuts) > 0:
        values = level_of(key, dims, cuts, -0.22, 0.18) * values
    return jnp.clip(values, min=-bound, max=bound).astype(kind)


def setup_inputs(seed: int = 0) -> dict:
    seeds = jax.random.split(jax.random.key(seed), 15)
    return {
        "out_grad": gaussian(seeds[0], (TOKENS, D), 0.1, 0.625, ((0, 4),)),
        "gate_pre": gaussian(seeds[1], (TOKENS, F), 1.5, 8.0, ((0, 4), (1, 8))),
        "up_pre": gaussian(seeds[2], (TOKENS, F), 1.0, 6.0, ((0, 4), (1, 8))),
        "rotated_codes": with_ends(jax.random.randint(seeds[3], (TOKENS, F), -127, 128), jax.random.fold_in(seeds[3], 1), -127, 127).astype(jnp.int32),
        "rotated_scale": jnp.clip(jnp.exp(math.log(0.02) - 2.30258502 * jax.random.uniform(seeds[4], (TOKENS,), jnp.float32) ** level_of(seeds[4], (TOKENS,), ((0, 4),), -0.2, 0.2)), 0.002, 0.02),
        "input_codes": with_ends(jax.random.randint(seeds[5], (TOKENS, D), -127, 128), jax.random.fold_in(seeds[5], 1), -127, 127).astype(jnp.int32),
        "input_scale": jnp.clip(jnp.exp(math.log(0.04) - 2.30258502 * jax.random.uniform(seeds[6], (TOKENS,), jnp.float32) ** level_of(seeds[6], (TOKENS,), ((0, 8),), -0.2, 0.2)), 0.004, 0.04),
        "gate_codes": with_ends(jax.random.randint(seeds[7], (D, F), -127, 128), jax.random.fold_in(seeds[7], 1), -127, 127).astype(jnp.int32),
        "gate_scale": jnp.clip(jnp.exp(math.log(0.0007) - 2.30258503 * jax.random.uniform(seeds[8], (F,), jnp.float32) ** level_of(seeds[8], (F,), ((0, 8),), -0.2, 0.2)), 7.000000186963007e-05, 0.0007),
        "up_codes": with_ends(jax.random.randint(seeds[9], (D, F), -127, 128), jax.random.fold_in(seeds[9], 1), -127, 127).astype(jnp.int32),
        "up_scale": jnp.clip(jnp.exp(math.log(0.0007) - 2.30258503 * jax.random.uniform(seeds[10], (F,), jnp.float32) ** level_of(seeds[10], (F,), ((0, 8),), -0.2, 0.2)), 7.000000186963007e-05, 0.0007),
        "down_codes": with_ends(jax.random.randint(seeds[11], (F, D), -127, 128), jax.random.fold_in(seeds[11], 1), -127, 127).astype(jnp.int32),
        "down_scale": jnp.clip(jnp.exp(math.log(0.0007) - 2.30258503 * jax.random.uniform(seeds[12], (D,), jnp.float32) ** level_of(seeds[12], (D,), ((0, 4),), -0.2, 0.2)), 7.000000186963007e-05, 0.0007),
        "sign_bits": with_ends(jax.random.randint(seeds[13], (F,), 0, 2), jax.random.fold_in(seeds[13], 1), 0, 1).astype(jnp.int32),
    }


def walsh_rows(values):
    row_count, width = values.shape
    half_width = 1
    while half_width < width:
        shaped = values.reshape(row_count, width // (2 * half_width), 2, half_width)
        lower_part = shaped[:, :, 0, :]
        upper_part = shaped[:, :, 1, :]
        values = jnp.stack([lower_part + upper_part, lower_part - upper_part], axis=2).reshape(row_count, width)
        half_width = half_width * 2
    return values

def reference(out_grad, gate_pre, up_pre, rotated_codes, rotated_scale, input_codes, input_scale, gate_codes, gate_scale, up_codes, up_scale, down_codes, down_scale, sign_bits):
    w_down = (down_codes.astype(jnp.float32) * down_scale[None, :]).astype(jnp.bfloat16)
    w_gate = (gate_codes.astype(jnp.float32) * gate_scale[None, :]).astype(jnp.bfloat16)
    w_up = (up_codes.astype(jnp.float32) * up_scale[None, :]).astype(jnp.bfloat16)
    x_input = (input_codes.astype(jnp.float32) * input_scale[:, None]).astype(jnp.bfloat16)
    rotated = (rotated_codes.astype(jnp.float32) * rotated_scale[:, None]).astype(jnp.bfloat16)

    def down_block(carry, block_index):
        first_col = (block_index * FEAT_BLOCK).astype(jnp.int32)
        grad_cols = lax.dynamic_slice_in_dim(out_grad, first_col, FEAT_BLOCK, 1)
        weight_cols = lax.dynamic_slice_in_dim(w_down, first_col, FEAT_BLOCK, 1)
        product = lax.dot_general(grad_cols, weight_cols, (((1,), (1,)), ((), ())), preferred_element_type=jnp.float32)
        rounded = lax.optimization_barrier(product.astype(jnp.bfloat16)).astype(jnp.float32)
        return (carry + rounded, None)
    rotated_grad, _ = lax.scan(down_block, jnp.zeros((TOKENS, F), jnp.float32), jnp.arange(N_DP, dtype=jnp.int32))
    signs = 1.0 - 2.0 * sign_bits.astype(jnp.float32)
    hidden_grad = signs[None, :] * walsh_rows(rotated_grad) / math.sqrt(F)
    gate_values = gate_pre.astype(jnp.float32)
    up_values = up_pre.astype(jnp.float32)
    sigmoid_gate = jax.nn.sigmoid(gate_values)
    gate_grad = (hidden_grad * up_values * sigmoid_gate * (1.0 + gate_values * (1.0 - sigmoid_gate))).astype(jnp.bfloat16)
    up_grad = (hidden_grad * gate_values * sigmoid_gate).astype(jnp.bfloat16)
    contract_rows = (((0,), (0,)), ((), ()))
    grad_down = lax.dot_general(rotated, out_grad, contract_rows, preferred_element_type=jnp.float32).astype(jnp.bfloat16)
    grad_gate = lax.dot_general(x_input, gate_grad, contract_rows, preferred_element_type=jnp.float32).astype(jnp.bfloat16)
    grad_up = lax.dot_general(x_input, up_grad, contract_rows, preferred_element_type=jnp.float32).astype(jnp.bfloat16)

    def unit_block(carry, block_index):
        first_col = (block_index * UNIT_BLOCK).astype(jnp.int32)
        gate_part = lax.dynamic_slice_in_dim(gate_grad, first_col, UNIT_BLOCK, 1)
        up_part = lax.dynamic_slice_in_dim(up_grad, first_col, UNIT_BLOCK, 1)
        gate_weight = lax.dynamic_slice_in_dim(w_gate, first_col, UNIT_BLOCK, 1)
        up_weight = lax.dynamic_slice_in_dim(w_up, first_col, UNIT_BLOCK, 1)
        contract_cols = (((1,), (1,)), ((), ()))
        term = lax.dot_general(gate_part, gate_weight, contract_cols, preferred_element_type=jnp.float32)
        term = term + lax.dot_general(up_part, up_weight, contract_cols, preferred_element_type=jnp.float32)
        return (carry + term, None)
    input_sum, _ = lax.scan(unit_block, jnp.zeros((TOKENS, D), jnp.float32), jnp.arange(N_TENSOR, dtype=jnp.int32))
    return (grad_down, grad_gate, grad_up, input_sum.astype(jnp.bfloat16))
```

```python
import math

import jax
import jax.numpy as jnp
from jax import lax
from jax.sharding import PartitionSpec as P


CONTRACT_COLS = (((1,), (1,)), ((), ()))
CONTRACT_ROWS = (((0,), (0,)), ((), ()))


def bit_count(value):
    return bin(value).count("1")


def hadamard_table(order, dtype):
    indices = lax.iota(jnp.int32, order)
    parity = lax.population_count(jnp.bitwise_and(indices[:, None], indices[None, :])) % 2
    return (1 - 2 * parity).astype(dtype)


def local_hadamard(values):
    rows, width = values.shape
    inner_size = min(width, 128)
    outer_size = width // inner_size
    shaped = values.reshape(rows, outer_size, inner_size)
    shaped = jnp.einsum(
        "rbk,kl->rbl",
        shaped,
        hadamard_table(inner_size, jnp.float32),
        precision=lax.Precision.HIGHEST,
    )
    shaped = jnp.einsum(
        "rbl,bc->rcl",
        shaped,
        hadamard_table(outer_size, jnp.float32),
        precision=lax.Precision.HIGHEST,
    )
    return shaped.reshape(values.shape)


def swap(values, axis, mask):
    size = lax.axis_size(axis)
    return lax.ppermute(values, axis, [(i, i ^ mask) for i in range(size)])


def axis_bits(axis):
    return [1 << b for b in range(lax.axis_size(axis).bit_length() - 1)]


def gather_xor(values, axis):
    bits = axis_bits(axis)
    parts = len(bits)
    rows = values.shape[0] // parts
    held = []
    for p in range(parts):
        held.append({0: values[p * rows : (p + 1) * rows]})
    for step in range(parts):
        arrived = []
        for p in range(parts):
            bit = bits[(p + step) % parts]
            own = sorted(held[p])
            sent = swap(jnp.concatenate([held[p][r] for r in own], 0), axis, bit)
            arrived.append({r ^ bit: sent[i * rows : (i + 1) * rows] for i, r in enumerate(own)})
        for p in range(parts):
            held[p].update(arrived[p])
    size = lax.axis_size(axis)
    return jnp.concatenate([held[p][r] for r in range(size) for p in range(parts)], 0)


def scatter_xor(shares, axis):
    bits = axis_bits(axis)
    parts = len(bits)
    size = lax.axis_size(axis)
    kept = [{r: shares(r, p) for r in range(size)} for p in range(parts)]
    for step in range(parts):
        arrived = []
        for p in range(parts):
            bit = bits[(p + step) % parts]
            out = sorted(r for r in kept[p] if r & bit)
            rows = kept[p][out[0]].shape[0]
            sent = swap(
                jnp.concatenate([kept[p][r].astype(jnp.bfloat16) for r in out], 0), axis, bit
            )
            arrived.append({r ^ bit: sent[i * rows : (i + 1) * rows] for i, r in enumerate(out)})
        for p in range(parts):
            kept[p] = {
                r: kept[p][r].astype(jnp.float32) + v.astype(jnp.float32)
                for r, v in arrived[p].items()
            }
    return jnp.concatenate([kept[p][0] for p in range(parts)], 0)


def local(
    out_grad,
    gate_pre,
    up_pre,
    rotated_codes,
    rotated_scale,
    input_codes,
    input_scale,
    gate_codes,
    gate_scale,
    up_codes,
    up_scale,
    down_codes,
    down_scale,
    sign_bits,
):
    f32, bf16 = jnp.float32, jnp.bfloat16
    n_dp, n_tensor = lax.axis_size("dp"), lax.axis_size("tensor")
    n_chips = n_tensor // 2
    d, t = lax.axis_index("dp"), lax.axis_index("tensor")
    chip, core = t // 2, t % 2
    group = out_grad.shape[0]
    half = group // 2
    unit_width, feats = down_codes.shape
    block = input_codes.shape[0]

    w_down = (down_codes.astype(f32) * down_scale[None, :]).astype(bf16)
    w_gate = (gate_codes.astype(f32) * gate_scale[None, :]).astype(bf16)
    w_up = (up_codes.astype(f32) * up_scale[None, :]).astype(bf16)
    x_input = (input_codes.astype(f32) * input_scale[:, None]).astype(bf16)
    rotated = (rotated_codes.astype(f32) * rotated_scale[:, None]).astype(bf16)

    halves = []
    for r in range(1, n_dp):
        piece = lax.dynamic_slice(out_grad, (core * half, (d ^ r) * feats), (half, feats))
        halves.append(swap(piece, "dp", r))
    mine = jnp.stack(halves)
    theirs = swap(mine, "tensor", 1)
    own_cols = lax.dynamic_slice(out_grad, (0, d * feats), (group, feats))
    first = jnp.where(core == 0, mine, theirs)
    second = jnp.where(core == 0, theirs, mine)
    away_rows = jnp.stack([first, second], 1).reshape((n_dp - 1) * group, feats)

    def product(rows):
        return lax.dot_general(rows, w_down, CONTRACT_COLS, preferred_element_type=f32).astype(bf16)

    away = product(away_rows)
    at_home = product(own_cols)
    parts = len(axis_bits("dp"))
    part_rows = group // parts

    def share(r, p):
        if r == 0:
            return at_home[p * part_rows : (p + 1) * part_rows]
        start = (r - 1) * group + p * part_rows
        return away[start : start + part_rows]

    rotated_grad = scatter_xor(share, "dp")

    spread = local_hadamard(rotated_grad).astype(bf16)
    core_sign = (1 - 2 * core).astype(f32)
    paired = swap(spread, "tensor", 1).astype(f32) + core_sign * spread.astype(f32)
    paired = paired.astype(bf16)
    set_rows = group // n_chips

    def sign_of(value):
        return (1 - 2 * (lax.population_count(value) % 2)).astype(f32)

    def row_set(values, index):
        return lax.dynamic_slice_in_dim(values, index * set_rows, set_rows, 0)

    arrived = [row_set(paired, chip)]
    for k in range(1, n_chips):
        arrived.append(swap(row_set(paired, chip ^ k), "tensor", 2 * k))
    arrived = [a.astype(f32) * sign_of(chip & k) for k, a in enumerate(arrived)]
    width = 1
    while width < n_chips:
        arrived = [
            arrived[k ^ width] - arrived[k] if k & width else arrived[k] + arrived[k ^ width]
            for k in range(n_chips)
        ]
        width *= 2
    mixed = [
        (a * (sign_of(chip) * sign_of(chip & k))).astype(bf16) for k, a in enumerate(arrived)
    ]
    mixed_grad = jnp.zeros((group, unit_width), bf16)
    for k in range(n_chips):
        rows = mixed[k] if k == 0 else swap(mixed[k], "tensor", 2 * k)
        mixed_grad = lax.dynamic_update_slice(mixed_grad, rows, ((chip ^ k) * set_rows, 0))

    full_width = unit_width * n_tensor
    signs = 1.0 - 2.0 * sign_bits.astype(f32)
    hidden_grad = signs[None, :] * mixed_grad.astype(f32) / math.sqrt(full_width)
    gate_values = gate_pre.astype(f32)
    up_values = up_pre.astype(f32)
    sigmoid_gate = jax.nn.sigmoid(gate_values)
    gate_grad = (
        hidden_grad * up_values * sigmoid_gate * (1.0 + gate_values * (1.0 - sigmoid_gate))
    ).astype(bf16)
    up_grad = (hidden_grad * gate_values * sigmoid_gate).astype(bf16)

    rotated_rows = gather_xor(rotated, "dp")
    grad_rows = jnp.concatenate([own_cols, away_rows], 0)
    grad_down = lax.dot_general(
        rotated_rows, grad_rows, CONTRACT_ROWS, preferred_element_type=f32
    ).astype(bf16)

    per_group = n_tensor // n_dp
    x_pieces = jnp.stack(
        [x_input] + [swap(x_input, "tensor", 2 * k) for k in range(1, n_chips)]
    )
    x_other = swap(x_pieces, "tensor", 1)
    x_rows = jnp.zeros((n_tensor * block, feats), bf16)

    def row_of(index):
        return (((index // per_group) ^ d) * per_group + index % per_group) * block

    for k in range(n_chips):
        for pieces, c in ((x_pieces, core), (x_other, 1 - core)):
            x_rows = lax.dynamic_update_slice(
                x_rows, pieces[k], (row_of(2 * (chip ^ k) + c), 0)
            )

    gate_rows = gather_xor(gate_grad, "dp")
    up_rows = gather_xor(up_grad, "dp")
    grad_gate = lax.dot_general(
        x_rows, gate_rows, CONTRACT_ROWS, preferred_element_type=f32
    ).astype(bf16)
    grad_up = lax.dot_general(
        x_rows, up_rows, CONTRACT_ROWS, preferred_element_type=f32
    ).astype(bf16)
    term = lax.dot_general(gate_rows, w_gate, CONTRACT_COLS, preferred_element_type=f32)
    term = term + lax.dot_general(up_rows, w_up, CONTRACT_COLS, preferred_element_type=f32)

    term = term.reshape(n_dp, per_group // 2, 2, block, feats)
    to_partner = lax.dynamic_index_in_dim(term, 1 - core, 2, False)
    kept = lax.dynamic_index_in_dim(term, core, 2, False)
    kept = kept + swap(to_partner.astype(bf16), "tensor", 1).astype(f32)
    kept = kept.reshape(n_chips, block, feats)

    def block_of(index):
        wide = per_group // 2
        return lax.dynamic_index_in_dim(
            kept, ((index // wide) ^ d) * wide + index % wide, 0, False
        )

    input_sum = block_of(chip)
    for k in range(1, n_chips):
        input_sum = input_sum + swap(block_of(chip ^ k).astype(bf16), "tensor", 2 * k).astype(f32)
    return grad_down, grad_gate, grad_up, input_sum.astype(bf16)


def solution(mesh):
    placed = (
        P("dp", None),
        P("dp", "tensor"),
        P("dp", "tensor"),
        P("dp", "tensor"),
        P("dp"),
        P("tensor", "dp"),
        P("tensor"),
        P("dp", "tensor"),
        P("tensor"),
        P("dp", "tensor"),
        P("tensor"),
        P("tensor", "dp"),
        P("dp"),
        P("tensor"),
    )
    return jax.shard_map(
        local,
        mesh=mesh,
        in_specs=placed,
        out_specs=(P("tensor", "dp"), P("dp", "tensor"), P("dp", "tensor"), P("tensor", "dp")),
        check_vma=False,
    )
```
